32 devices in a mesh: seq: 2 (over y), track: 16 (over z, x, core).
Axes of the slice: x: 2, y: 2, z: 4, core: 2. Of those that a mesh axis runs over, the one named last changes fastest.
Arguments:
- inputs: bfloat16 [32, 1024, 768], P('track', 'seq'), may hold values from -15 to 15
- conv_weight: bfloat16 [3, 768, 384], replicated, may hold values from -0.125 to 0.125
- norm1_gain: float32 [384], replicated, may hold values from 0.25 to 1.75
- norm1_shift: float32 [384], replicated, may hold values from -3 to 3
- mix_weight: bfloat16 [384, 768], replicated, may hold values from -0.3125 to 0.3125
- norm2_gain: float32 [768], replicated, may hold values from 0.25 to 1.75
- norm3_gain: float32 [768], replicated, may hold values from 0.25 to 1.75
- norm3_shift: float32 [768], replicated, may hold values from -3 to 3
- point_weight: bfloat16 [768, 1536], replicated, may hold values from -0.21875 to 0.21875
- point_bias: float32 [1536], replicated, may hold values from -3 to 3
- head_weight: bfloat16 [1536, 5376], P(None, 'track'), may hold values from -0.15625 to 0.15625
- head_bias: bfloat16 [5376], P('track'), may hold values from -3 to 3
- targets: bfloat16 [32, 1024, 5376], P(None, 'seq', 'track'), may hold values from 0 to 4
- lengths: int32 [32], replicated, may hold values from 256 to 1024, as said below
- track_mask: int32 [5376], P('track'), may hold values 0 or 1
Outputs:
- loss: float32 [], replicated
- inputs_grad: float32 [32, 1024, 768], P('track', 'seq')
- conv_weight_grad: float32 [3, 768, 384], replicated
- norm1_gain_grad: float32 [384], replicated
- norm1_shift_grad: float32 [384], replicated
- mix_weight_grad: float32 [384, 768], replicated
- norm2_gain_grad: float32 [768], replicated
- norm3_gain_grad: float32 [768], replicated
- norm3_shift_grad: float32 [768], replicated
- point_weight_grad: float32 [768, 1536], replicated
- point_bias_grad: float32 [1536], replicated
- head_weight_grad: float32 [1536, 5376], P(None, 'track')
- head_bias_grad: float32 [5376], P('track')
The draws below stay inside these ranges and needn't reach their ends.
Inputs may be any that keep to these rules, and one draw needn't show every extreme that they name: `lengths`: valid bins are the first ones of a window; the rest are padding.
All inputs are finite; a program needn't handle non-finite values. No bound on the sum of `track_mask` on one device may be relied on, other than what follows from the above.
Results may differ from the reference program's by a relative error of at most 0.007.
Values may be sent and summed in bfloat16 or wider, within the bound.
No kernel may reach another device: no remote copies, remote signals or barrier semaphores. Data moves between devices by JAX's collectives and lax.ppermute only.
A program may use at most 320 MiB of HBM per device.

```python
import jax
import jax.numpy as jnp
from jax import lax

TOWER_CHANNELS = 768
F = 384
H = 1536
TRACKS = 5376
WINDOW_BINS = 1024
DILATION_STEP = 58
WINDOWS = 32


def draw_inputs(key, part):
    first = jax.random.fold_in(key, 0)
    base = jnp.clip(jax.random.normal(first, (WINDOWS, WINDOW_BINS, TOWER_CHANNELS), jnp.float32), -5.0, 5.0)
    windows_at = jnp.arange(WINDOWS, dtype=jnp.float32) / (WINDOWS - 1)
    bins_at = jnp.arange(WINDOW_BINS, dtype=jnp.float32) / (WINDOW_BINS - 1)
    growth = jnp.exp(0.5 * jnp.log(3.0) * (windows_at[:, None] + bins_at[None, :]))
    return (base * growth[:, :, None]).astype(jnp.bfloat16)


def draw_lengths(key, part):
    first, second, third = jax.random.split(jax.random.fold_in(key, 7), 3)
    values = jax.random.randint(first, (WINDOWS,), WINDOW_BINS // 4, WINDOW_BINS + 1)
    longest = jax.random.randint(second, (), 0, WINDOWS)
    values = values.at[longest].set(WINDOW_BINS)
    shortest = (longest + 1 + jax.random.randint(third, (), 0, WINDOWS - 1)) % WINDOWS
    return values.at[shortest].set(WINDOW_BINS // 4).astype(jnp.int32)


def set_ends(drawn, own_key, smallest, high):
    longest = drawn.shape.index(max(drawn.shape))
    spots = []
    for shift in (0, 1):
        where = [jax.random.randint(jax.random.fold_in(own_key, axis), (), 0, length) for axis, length in enumerate(drawn.shape)]
        where[longest] = (where[longest] + shift) % drawn.shape[longest]
        spots.append(tuple(where))
    return drawn.at[spots[0]].set(smallest).at[spots[1]].set(high)


def block_scale(own_key, extent, cuts, least, high):
    def one(dim, parts):
        heights = jax.random.uniform(jax.random.fold_in(jax.random.fold_in(own_key, 6), dim), (parts,), jnp.float32, least / len(cuts), high / len(cuts))
        return jnp.repeat(jnp.exp(heights), extent[dim] // parts).reshape((-1,) + (1,) * (len(extent) - dim - 1))

    factor_of = one(*cuts[0])
    for cut in cuts[1:]:
        factor_of = factor_of * one(*cut)
    return factor_of


def normal_values(stream_key, shape, spread, most, shards=(), held_as=jnp.bfloat16):
    factor_of = block_scale(stream_key, shape, shards, -0.22, 0.18) if shards else 1.0
    array = jax.random.normal(stream_key, shape, jnp.float32) * spread * factor_of
    return jnp.minimum(jnp.maximum(array, -most), most).astype(held_as)


def setup_inputs(seed: int = 0) -> dict:
    key_list = jax.random.split(jax.random.key(seed), 16)
    return {
        "inputs": draw_inputs(jax.random.fold_in(key_list[15], 71), 0),
        "conv_weight": normal_values(key_list[1], (3, TOWER_CHANNELS, F), (3 * TOWER_CHANNELS) ** -0.5, 0.125),
        "norm1_gain": jnp.clip(1.0 + 0.15 * jax.random.normal(key_list[2], (F,), jnp.float32), 0.25, 1.75),
        "norm1_shift": normal_values(key_list[3], (F,), 0.5, 3.0, (), jnp.float32),
        "mix_weight": normal_values(key_list[4], (F, TOWER_CHANNELS), F ** -0.5, 0.3125),
        "norm2_gain": jnp.clip(1.0 + 0.15 * jax.random.normal(key_list[5], (TOWER_CHANNELS,), jnp.float32), 0.25, 1.75),
        "norm3_gain": jnp.clip(1.0 + 0.15 * jax.random.normal(key_list[6], (TOWER_CHANNELS,), jnp.float32), 0.25, 1.75),
        "norm3_shift": normal_values(key_list[7], (TOWER_CHANNELS,), 0.5, 3.0, (), jnp.float32),
        "point_weight": normal_values(key_list[8], (TOWER_CHANNELS, H), TOWER_CHANNELS ** -0.5, 0.21875),
        "point_bias": normal_values(key_list[9], (H,), 0.5, 3.0, (), jnp.float32),
        "head_weight": normal_values(key_list[10], (H, TRACKS), H ** -0.5, 0.15625, ((1, 16),)),
        "head_bias": normal_values(key_list[11], (TRACKS,), 0.5, 3.0, ((0, 16),)),
        "targets": jnp.clip(4.0 * jax.random.uniform(key_list[12], (WINDOWS, WINDOW_BINS, TRACKS), jnp.float32) ** block_scale(key_list[12], (WINDOWS, WINDOW_BINS, TRACKS), ((1, 2), (2, 16)), -0.2, 0.2), 0.0, 4.0).astype(jnp.bfloat16),
        "lengths": draw_lengths(jax.random.fold_in(key_list[15], 71), 0),
        "track_mask": set_ends((jax.random.randint(key_list[14], (TRACKS,), 0, 64) < 63).astype(jnp.int32), jax.random.fold_in(key_list[14], 1), 0, 1),
    }


EPSILON = 1e-05
PRECISE = lax.Precision.HIGHEST

@jax.custom_vjp
def low(v):
    return lax.optimization_barrier(v.astype(jnp.bfloat16)).astype(jnp.float32)

@jax.custom_vjp
def low_back(v):
    return v

def low_keep(v):
    return (low(v), None)

def low_pass(kept, grad):
    return (grad,)

def back_keep(v):
    return (v, None)

def back_low(kept, grad):
    return (low(grad),)
low.defvjp(low_keep, low_pass)
low_back.defvjp(back_keep, back_low)

def norm_apply(values, gain, shift):
    col_mean = lax.optimization_barrier(jnp.mean(values, axis=0))
    col_var = lax.optimization_barrier(jnp.mean(values * values, axis=0)) - col_mean * col_mean
    return (values - col_mean) * lax.rsqrt(col_var + EPSILON) * gain + shift

def reference(inputs, conv_weight, norm1_gain, norm1_shift, mix_weight, norm2_gain, norm3_gain, norm3_shift, point_weight, point_bias, head_weight, head_bias, targets, lengths, track_mask):
    observed = targets.astype(jnp.float32)
    tracks_ok = track_mask > 0
    places = jnp.arange(WINDOW_BINS, dtype=jnp.int32)
    count_of_rows = WINDOWS * WINDOW_BINS
    loss_scale = 1.0 / (WINDOWS * WINDOW_BINS * TRACKS)

    def forward(source_rows, conv_w, gain_one, shift_one, mix_w, gain_two, gain_three, shift_three, point_w, point_b, head_w, head_b):
        border_padded = jnp.pad(source_rows, ((0, 0), (DILATION_STEP, DILATION_STEP), (0, 0)))
        conv_out = jnp.zeros((count_of_rows, F), jnp.float32)
        for kernel_offset in range(3):
            offset_rows = border_padded[:, kernel_offset * DILATION_STEP:kernel_offset * DILATION_STEP + WINDOW_BINS].reshape(count_of_rows, TOWER_CHANNELS)
            conv_out = conv_out + jnp.dot(offset_rows, conv_w[kernel_offset], precision=PRECISE)
        conv_out = low_back(conv_out)
        first_act = low(jax.nn.gelu(norm_apply(conv_out, gain_one, shift_one)))
        mix_out = low_back(jnp.dot(first_act, mix_w, precision=PRECISE))
        stream = source_rows.reshape(count_of_rows, TOWER_CHANNELS) + norm_apply(mix_out, gain_two, 0.0)
        third_act = low(jax.nn.gelu(norm_apply(stream, gain_three, shift_three)))
        point_out = low_back(jnp.dot(third_act, point_w, precision=PRECISE) + point_b)
        hidden = low(jax.nn.gelu(point_out)).reshape(WINDOWS, WINDOW_BINS, H)

        def head_block(window_block):
            rows_here, observed_here, valid_here = window_block
            logits = low_back(jnp.dot(rows_here, head_w, precision=PRECISE) + head_b)
            predicted = jax.nn.softplus(logits)
            kept_mask = (places < valid_here)[:, None] & tracks_ok[None, :]
            return jnp.sum(jnp.where(kept_mask, predicted - observed_here * jnp.log(predicted), 0.0))
        totals = lax.map(jax.checkpoint(head_block), (hidden, observed, lengths))
        return jnp.sum(totals) * loss_scale
    primals = (inputs.astype(jnp.float32), conv_weight.astype(jnp.float32), norm1_gain, norm1_shift, mix_weight.astype(jnp.float32), norm2_gain, norm3_gain, norm3_shift, point_weight.astype(jnp.float32), point_bias, head_weight.astype(jnp.float32), head_bias.astype(jnp.float32))
    loss, pullback = jax.vjp(forward, *primals)
    grads = pullback(jnp.ones((), jnp.float32))
    return (loss, grads[0], grads[1], grads[2], grads[3], grads[4], grads[5], grads[6], grads[7], grads[8], grads[9], grads[10], grads[11])
```

```python
import jax
import jax.numpy as jnp
from jax import lax
from jax.sharding import PartitionSpec as P

TRACKS = 5376
WINDOW_BINS = 1024
DILATION_STEP = 58


EPSILON = 1e-05


def swap(block, axis, bits):
    count = lax.axis_size(axis)
    return lax.ppermute(block, axis, [(i, i ^ bits) for i in range(count)])


def axis_bits(axis):
    return [1 << b for b in range(lax.axis_size(axis).bit_length() - 1)]


def small_sum(values):
    for axis in ("track", "seq"):
        for bits in axis_bits(axis):
            values = values + swap(values, axis, bits)
    return values


def halves(block, bit):
    half = block.shape[0] // 2
    mine = lax.dynamic_slice_in_dim(block, bit * half, half, 0)
    other = lax.dynamic_slice_in_dim(block, (1 - bit) * half, half, 0)
    return mine, other


def joined(mine, other, bit):
    return jnp.where(
        bit == 0, jnp.concatenate([mine, other]), jnp.concatenate([other, mine])
    )


def sum_order():
    track, seq = lax.axis_index("track"), lax.axis_index("seq")
    order = [("track", 1, track & 1)]
    order += [("seq", b, (seq // b) & 1) for b in axis_bits("seq")]
    order += [("track", 2, (track // 2) & 1)]
    order += [("track", b, (track // b) & 1) for b in axis_bits("track")[2:][::-1]]
    return order


def weight_sum(part):
    order = sum_order()
    block = part
    for axis, bits, bit in order:
        mine, other = halves(block, bit)
        block = mine + swap(other.astype(jnp.bfloat16), axis, bits).astype(jnp.float32)
    block = block.astype(jnp.bfloat16)
    for axis, bits, bit in order[::-1]:
        block = joined(block, swap(block, axis, bits), bit)
    return block.astype(jnp.float32)


def seq_all(block):
    seq = lax.axis_index("seq")
    for bits in axis_bits("seq"):
        block = joined(block, swap(block, "seq", bits), (seq // bits) & 1)
    return block


def seq_part(block):
    seq = lax.axis_index("seq")
    for bits in axis_bits("seq")[::-1]:
        mine, other = halves(block, (seq // bits) & 1)
        block = mine + swap(other.astype(jnp.bfloat16), "seq", bits).astype(jnp.float32)
    return block


def padded(block, width):
    count = lax.axis_size("seq")
    forward = [(i, i + 1) for i in range(count - 1)]
    backward = [(target, source) for source, target in forward]
    bins = block.shape[1]
    low = lax.ppermute(lax.slice_in_dim(block, bins - width, None, axis=1), "seq", forward)
    high = lax.ppermute(lax.slice_in_dim(block, 0, width, axis=1), "seq", backward)
    return jnp.concatenate([low, block, high], axis=1)


def gelu_back(before, upstream):
    _, pullback = jax.vjp(jax.nn.gelu, before)
    return pullback(upstream)[0]


def head_loss(logits, observed, kept_mask, loss_scale):
    predicted = jax.nn.softplus(logits)
    loss_part = jnp.sum(jnp.where(kept_mask, predicted - observed * jnp.log(predicted), 0.0))
    slopes = (
        jnp.where(kept_mask, jax.nn.sigmoid(logits) * (1.0 - observed / predicted), 0.0)
        * loss_scale
    )
    return (loss_part, slopes.astype(jnp.bfloat16))


def outer_sum(left, right):
    return lax.dot_general(
        left, right, (((0,), (0,)), ((), ())), preferred_element_type=jnp.float32
    )


def times_transpose(left, right):
    return lax.dot_general(
        left, right, (((1,), (1,)), ((), ())), preferred_element_type=jnp.float32
    )


def spread_of(total, square_total, bin_total):
    col_mean = total / bin_total
    col_var = square_total / bin_total - col_mean * col_mean
    return col_mean, lax.rsqrt(col_var + EPSILON)


def shards(
    inputs,
    conv_weight,
    norm1_gain,
    norm1_shift,
    mix_weight,
    norm2_gain,
    norm3_gain,
    norm3_shift,
    point_weight,
    point_bias,
    head_weight,
    head_bias,
    targets,
    lengths,
    track_mask,
):
    window_shard, shard_bins, channel_width = inputs.shape
    rows = window_shard * shard_bins
    track_local = head_weight.shape[1]
    track_count = lax.axis_size("track")
    chips = track_count // 2
    pair_windows = 2 * window_shard
    track = lax.axis_index("track")
    chip, core = track // 2, track & 1
    seq = lax.axis_index("seq")
    bin_total = float(rows * lax.axis_size("seq") * track_count)
    loss_scale = 1.0 / (targets.shape[0] * WINDOW_BINS * TRACKS)
    bf16 = jnp.bfloat16

    part_rows = head_weight.shape[0] // lax.axis_size("seq")
    head_part = lax.dynamic_slice_in_dim(head_weight, seq * part_rows, part_rows, 0)
    heads = {0: head_weight}
    far = list(range(2, chips, 2))
    for k in far:
        heads[k] = swap(head_part, "track", 2 * k)
    seen = {}
    for k in [k for k in range(chips - 1, 0, -1)] + [0]:
        block = lax.dynamic_slice_in_dim(targets, (chip ^ k) * pair_windows, pair_windows, 0)
        seen[k] = swap(block, "track", 2 * k) if k else block
    for k in far:
        heads[k] = seq_all(heads[k])
    for k in [0] + far:
        heads[k + 1] = swap(heads[k], "track", 2)
    small_tracks = jnp.stack([head_bias.astype(jnp.float32), track_mask.astype(jnp.float32)])
    all_small = lax.all_to_all(
        jnp.broadcast_to(small_tracks, (track_count,) + small_tracks.shape),
        "track", 0, 0, tiled=True,
    ).reshape(chips, 2, 2, track_local)
    my_small = lax.dynamic_index_in_dim(all_small, core, 1, keepdims=False)

    rows_in = inputs.reshape(rows, channel_width)
    padded_input = padded(inputs, DILATION_STEP)
    taps = [
        padded_input[:, t * DILATION_STEP : t * DILATION_STEP + shard_bins].reshape(
            rows, channel_width
        )
        for t in range(3)
    ]
    conv_out = jnp.zeros((rows, conv_weight.shape[2]), jnp.float32)
    for t in range(3):
        conv_out = conv_out + jnp.dot(taps[t], conv_weight[t], preferred_element_type=jnp.float32)
    sums = small_sum(jnp.stack([jnp.sum(conv_out, axis=0), jnp.sum(conv_out * conv_out, axis=0)]))
    first_mean, first_spread = spread_of(sums[0], sums[1], bin_total)
    first_unit = (conv_out - first_mean) * first_spread
    first_norm = first_unit * norm1_gain + norm1_shift
    first_act = jax.nn.gelu(first_norm).astype(bf16)
    mix_out = jnp.dot(first_act, mix_weight, preferred_element_type=jnp.float32)
    wide = rows_in.astype(jnp.float32)
    sums = small_sum(
        jnp.stack(
            [
                jnp.sum(mix_out, axis=0),
                jnp.sum(mix_out * mix_out, axis=0),
                jnp.sum(wide, axis=0),
                jnp.sum(wide * wide, axis=0),
                jnp.sum(wide * mix_out, axis=0),
            ]
        )
    )
    second_mean, second_spread = spread_of(sums[0], sums[1], bin_total)
    unit2_sum = (sums[0] - bin_total * second_mean) * second_spread
    unit2_square = (sums[1] - bin_total * second_mean * second_mean) * second_spread * second_spread
    wide_unit2 = (sums[4] - second_mean * sums[2]) * second_spread
    stream_sum = sums[2] + norm2_gain * unit2_sum
    stream_square = (
        sums[3] + 2.0 * norm2_gain * wide_unit2 + norm2_gain * norm2_gain * unit2_square
    )
    third_mean, third_spread = spread_of(stream_sum, stream_square, bin_total)
    unit3_sum = (stream_sum - bin_total * third_mean) * third_spread
    unit3_unit2 = (wide_unit2 + norm2_gain * unit2_square - third_mean * unit2_sum) * third_spread
    second_unit = (mix_out - second_mean) * second_spread
    third_unit = (wide + second_unit * norm2_gain - third_mean) * third_spread
    third_norm = third_unit * norm3_gain + norm3_shift
    third_act = jax.nn.gelu(third_norm).astype(bf16)
    point_out = jnp.dot(third_act, point_weight, preferred_element_type=jnp.float32) + point_bias
    hidden = jax.nn.gelu(point_out).astype(bf16)
    hidden_pair = joined(hidden, swap(hidden, "track", 1), core)

    pair_lengths = lax.dynamic_slice_in_dim(lengths, chip * pair_windows, pair_windows, 0)
    seq_place = seq * shard_bins + jnp.arange(shard_bins, dtype=jnp.int32)
    bins_ok = seq_place[None, :] < pair_lengths[:, None]
    hidden_grad = jnp.zeros((pair_windows * shard_bins, hidden.shape[1]), jnp.float32)
    loss_part = jnp.zeros((), jnp.float32)
    bias_parts = []
    own = None
    for kz in range(0, chips, 2):
        weight = jnp.concatenate([heads[kz], heads[kz + 1]], axis=1)
        observed = jnp.concatenate([seen[kz], seen[kz + 1]], axis=2).astype(jnp.float32)
        small = jnp.concatenate(
            [
                lax.dynamic_index_in_dim(my_small, chip ^ kz, 0, keepdims=False),
                lax.dynamic_index_in_dim(my_small, chip ^ (kz + 1), 0, keepdims=False),
            ],
            axis=1,
        )
        logits = jnp.dot(hidden_pair, weight, preferred_element_type=jnp.float32) + small[0]
        logits = logits.reshape(pair_windows, shard_bins, -1)
        kept_mask = bins_ok[:, :, None] & (small[1] > 0.0)[None, None, :]
        loss_here, slopes = head_loss(logits, observed, kept_mask, loss_scale)
        loss_part = loss_part + loss_here
        slopes = slopes.reshape(pair_windows * shard_bins, -1)
        bias_parts.append(jnp.sum(slopes.astype(jnp.float32), axis=0).reshape(2, track_local))
        hidden_grad = hidden_grad + times_transpose(slopes, weight)
        weight_part = outer_sum(hidden_pair, slopes)
        near = weight_part[:, :track_local] + swap(
            weight_part[:, track_local:].astype(bf16), "track", 2
        ).astype(jnp.float32)
        near = seq_part(near)
        if kz:
            near = swap(near.astype(bf16), "track", 2 * kz).astype(jnp.float32)
        own = near if own is None else own + near
    head_w_grad = seq_all(own.astype(bf16)).astype(jnp.float32)
    bias_parts = jnp.concatenate(bias_parts)[chip ^ jnp.arange(chips)]
    bias_full = jnp.where(
        (jnp.arange(2) == core)[None, :, None], bias_parts[:, None, :], 0.0
    ).reshape(-1)

    hidden_mine, hidden_other = halves(hidden_grad, core)
    hidden_mine = hidden_mine + swap(hidden_other.astype(bf16), "track", 1).astype(jnp.float32)
    point_grad = gelu_back(point_out, hidden_mine).astype(bf16)
    point_w_grad = weight_sum(outer_sum(third_act, point_grad))
    point_b_part = jnp.sum(point_grad.astype(jnp.float32), axis=0)
    third_grad = gelu_back(third_norm, times_transpose(point_grad, point_weight))
    widths = [channel_width] * 3 + [point_b_part.shape[0], bias_full.shape[0], 1]
    packed = jnp.concatenate(
        [
            jnp.sum(third_grad, axis=0),
            jnp.sum(third_grad * third_unit, axis=0),
            jnp.sum(third_grad * second_unit, axis=0),
            point_b_part,
            bias_full,
            loss_part.reshape(1),
        ]
    )
    packed = small_sum(packed)
    pieces, start = [], 0
    for width in widths:
        pieces.append(lax.slice_in_dim(packed, start, start + width))
        start += width
    shift3_grad, gain3_grad, third_unit2, point_b_grad, bias_all, loss_all = pieces
    scale3 = norm3_gain * third_spread
    stream_grad = scale3 * (
        third_grad - shift3_grad / bin_total - third_unit * (gain3_grad / bin_total)
    )
    stream_total = scale3 * (
        shift3_grad - shift3_grad - unit3_sum * (gain3_grad / bin_total)
    )
    gain2_grad = scale3 * (
        third_unit2
        - unit2_sum * (shift3_grad / bin_total)
        - unit3_unit2 * (gain3_grad / bin_total)
    )
    mix_grad = (norm2_gain * second_spread) * (
        stream_grad - stream_total / bin_total - second_unit * (gain2_grad / bin_total)
    )
    mix_low = mix_grad.astype(bf16)
    mix_w_grad = weight_sum(outer_sum(mix_low, first_act)).T
    first_grad = gelu_back(first_norm, times_transpose(mix_low, mix_weight))
    sums = small_sum(
        jnp.stack([jnp.sum(first_grad, axis=0), jnp.sum(first_grad * first_unit, axis=0)])
    )
    shift1_grad, gain1_grad = sums[0], sums[1]
    conv_grad = (norm1_gain * first_spread) * (
        first_grad - shift1_grad / bin_total - first_unit * (gain1_grad / bin_total)
    )
    conv_low = conv_grad.astype(bf16)
    conv_w_grad = weight_sum(
        jnp.concatenate([outer_sum(taps[t], conv_low) for t in range(3)])
    ).reshape(conv_weight.shape)
    border = padded(conv_low.reshape(window_shard, shard_bins, -1), DILATION_STEP)
    input_grad = stream_grad
    for t in range(3):
        moved = border[
            :, (2 - t) * DILATION_STEP : (2 - t) * DILATION_STEP + shard_bins
        ].reshape(rows, -1)
        input_grad = input_grad + times_transpose(moved, conv_weight[t])
    return (
        loss_all[0] * loss_scale,
        input_grad.reshape(inputs.shape),
        conv_w_grad,
        gain1_grad,
        shift1_grad,
        mix_w_grad,
        gain2_grad,
        gain3_grad,
        shift3_grad,
        point_w_grad,
        point_b_grad,
        head_w_grad,
        lax.dynamic_slice_in_dim(bias_all, track * track_local, track_local),
    )


def solution(mesh):
    placed = (
        P("track", "seq", None),
        P(),
        P(),
        P(),
        P(),
        P(),
        P(),
        P(),
        P(),
        P(),
        P(None, "track"),
        P("track"),
        P(None, "seq", "track"),
        P(),
        P("track"),
    )
    return jax.shard_map(
        shards,
        mesh=mesh,
        in_specs=placed,
        out_specs=(
            P(),
            P("track", "seq", None),
            P(),
            P(),
            P(),
            P(),
            P(),
            P(),
            P(),
            P(),
            P(),
            P(None, "track"),
            P("track"),
        ),
        check_vma=False,
    )
```
